32 devices in a mesh: section: 2 (over x), tile: 16 (over z, y, core).
Axes of the slice: x: 2, y: 2, z: 4, core: 2. Of those that a mesh axis runs over, the one named last changes fastest.
Arguments:
- features: bfloat16 [16, 12, 1024, 128], P('tile', 'section'), may hold values from -6 to 6
- conv_weight: bfloat16 [5, 5, 128, 128], replicated, may hold values from -0.109375 to 0.109375
- head_weight: bfloat16 [128, 16], replicated, may hold values from -0.5 to 0.5
- kernels: bfloat16 [128, 1024, 2048], P('tile'), may hold values from -0.015625 to 0.015625
- source_weights: float32 [8], replicated, may hold values from 0.3 to 3
Outputs:
- intensity: float32 [16, 12, 1024], P('tile', 'section')
The draws below stay inside these ranges and needn't reach their ends.
All inputs are finite; a program needn't handle non-finite values.
Results may differ from the reference program's by a relative error of at most 0.0018.
Values may be sent and summed in bfloat16 or wider, within the bound.
A program may use at most 128 MiB of HBM per device.

```python
import math
import jax
import jax.numpy as jnp
from jax import lax

C = 128
K = 16
ANG = 8
W = 1024
TILES = 16
ROWS = 12


def steps_of(stream_key, shape, split, least, largest):
    gain = 1.0
    for axis_at, shards_of in split:
        draws = jax.random.uniform(jax.random.fold_in(jax.random.fold_in(stream_key, 6), axis_at), (shards_of,), jnp.float32, least / len(split), largest / len(split))
        gain = gain * jnp.repeat(jnp.exp(draws), shape[axis_at] // shards_of).reshape((-1,) + (1,) * (len(shape) - 1 - axis_at))
    return gain


def centred(rng, extent, scale, bound, shards=(), held_as=jnp.bfloat16):
    values = scale * jax.random.normal(rng, extent, jnp.float32)
    if shards:
        values = values * steps_of(rng, extent, shards, -0.22, 0.18)
    return jnp.clip(values, -bound, bound).astype(held_as)


def setup_inputs(seed: int = 0) -> dict:
    keys = jax.random.split(jax.random.key(seed), 6)
    return {
        "features": centred(keys[0], (TILES, ROWS, W, C), 1.0, 6.0, ((0, 16), (1, 2))),
        "conv_weight": centred(keys[1], (5, 5, C, C), (25 * C) ** -0.5, 0.109375),
        "head_weight": centred(keys[2], (C, 2 * ANG), C ** -0.5, 0.5),
        "kernels": centred(keys[3], (ANG * K, W, 2 * W), (W * K * ANG) ** -0.5, 0.015625, ((0, 16),)),
        "source_weights": jnp.clip(jnp.exp(jax.random.uniform(keys[4], (ANG,), jnp.float32, math.log(0.3), math.log(3.0))), 0.3, 3.0),
    }


def socs_image(field, operators):
    pixels = field.shape[-1]
    product = jnp.einsum('prw,kwv->pkrv', field.astype(jnp.float32), operators.astype(jnp.float32))
    real_part = product[0, :, :, :pixels] - product[1, :, :, pixels:]
    imag_part = product[0, :, :, pixels:] + product[1, :, :, :pixels]
    return jnp.sum(real_part * real_part + imag_part * imag_part, axis=0)


def reference(features, conv_weight, head_weight, kernels, source_weights):
    operators = kernels.reshape(ANG, K, kernels.shape[1], kernels.shape[2])

    def one_tile(window):
        preact = lax.conv_general_dilated(window[None], conv_weight, (1, 1), ((4, 4), (4, 4)), rhs_dilation=(2, 2), dimension_numbers=('NHWC', 'HWIO', 'NHWC'), preferred_element_type=jnp.float32)[0]
        hidden = jax.nn.gelu(preact, approximate=True).astype(jnp.bfloat16)
        near_field = jnp.einsum('rwc,cd->drw', hidden.astype(jnp.float32), head_weight.astype(jnp.float32)).astype(jnp.bfloat16)
        near_field = near_field.reshape(ANG, 2, near_field.shape[1], near_field.shape[2])
        running = jnp.zeros(near_field.shape[2:], jnp.float32)
        for angle_id in range(ANG):
            running = running + source_weights[angle_id] * socs_image(near_field[angle_id], operators[angle_id])
        return running
    return lax.map(one_tile, features)
```

```python
import functools

import jax
import jax.numpy as jnp
from jax import lax
from jax.experimental import pallas as pl
from jax.experimental.pallas import tpu as pltpu
from jax.sharding import PartitionSpec as P

ANG = 8
TAPS = 5
CHUNKS = 4
PAD = 16
BUNCH = 4
MESH = pl.DeviceIdType.MESH


def kernel(tiles, groups, feat, conv_w, head_t, operators, source_w, out_ref,
           x_ref, w_ref, l_ref, ns_ref, nr_ref, ef_ref, e_ref, g_ref, s_ref, r_ref, rr_ref,
           own_sem, w_sem, g_sem, halo_send, halo_recv, near_send, near_recv, near_own,
           ret_send, ret_recv, ret_own):
    sec = lax.axis_index("section")
    me = lax.axis_index("tile")
    half, pixels, chans = feat.shape[0], feat.shape[2], feat.shape[3]
    units = 2 * half
    pairs = units // 2
    kers = operators.shape[0]
    cw = pixels // CHUNKS
    span = TAPS * 2 * chans
    wide = 2 * chans

    own = pltpu.make_async_copy(
        feat.at[:, sec], x_ref.at[pl.ds(sec * half, half), pl.ds(PAD, pixels), :], own_sem)
    own.start()
    w_copies = []
    for d in range(3):
        for si in range(2):
            for so in range(2):
                tap = 2 * d + si - so
                if 0 <= tap < TAPS:
                    copy = pltpu.make_async_copy(
                        conv_w.at[tap],
                        w_ref.at[d, :, pl.ds(si * chans, chans), pl.ds(so * chans, chans)],
                        w_sem.at[len(w_copies)])
                    copy.start()
                    w_copies.append(copy)
                else:
                    w_ref[d, :, si * chans:(si + 1) * chans, so * chans:(so + 1) * chans] = jnp.zeros(
                        (TAPS, chans, chans), w_ref.dtype)

    barrier = pltpu.get_barrier_semaphore()

    def greet(i, carry):
        peer = lax.rem(me + i, tiles)
        pl.semaphore_signal(barrier, inc=1, device_id=(sec, peer), device_id_type=MESH)
        pl.semaphore_signal(barrier, inc=1, device_id=(1 - sec, peer), device_id_type=MESH)
        return carry

    pl.semaphore_signal(barrier, inc=1, device_id=(1 - sec, me), device_id_type=MESH)
    lax.fori_loop(1, tiles, greet, 0)
    pl.semaphore_wait(barrier, 2 * tiles - 1)

    halos = []
    for c in range(CHUNKS):
        lo = 0 if c == 0 else c * cw + PAD
        hi = pixels if c == CHUNKS - 1 else (c + 1) * cw + PAD
        copy = pltpu.make_async_remote_copy(
            src_ref=feat.at[:, 1 - sec, pl.ds(lo, hi - lo), :],
            dst_ref=x_ref.at[pl.ds(sec * half, half), pl.ds(PAD + lo, hi - lo), :],
            send_sem=halo_send.at[c], recv_sem=halo_recv.at[c],
            device_id=(1 - sec, me), device_id_type=MESH)
        copy.start()
        halos.append(copy)

    g_copies = []
    for k in range(kers):
        copy = pltpu.make_async_copy(operators.at[k], g_ref.at[k], g_sem.at[k])
        copy.start()
        g_copies.append(copy)

    edge = jnp.zeros((units, PAD, chans), x_ref.dtype)
    x_ref[:, 0:PAD, :] = edge
    x_ref[:, PAD + pixels:, :] = edge
    own.wait()
    for copy in w_copies:
        copy.wait()

    def near_copy(c, peer):
        return pltpu.make_async_remote_copy(
            src_ref=ns_ref.at[c, peer // groups], dst_ref=nr_ref.at[c, me],
            send_sem=near_send.at[c, peer], recv_sem=near_recv.at[c, me],
            device_id=(sec, peer), device_id_type=MESH)

    def near_arrival(c, peer):
        return pltpu.make_async_remote_copy(
            src_ref=ns_ref.at[c, 0], dst_ref=nr_ref.at[c, peer],
            send_sem=near_send.at[c, peer], recv_sem=near_recv.at[c, peer],
            device_id=(sec, peer), device_id_type=MESH)

    def conv_chunk(c, carry):
        for cc in range(CHUNKS):
            @pl.when(c == cc)
            def _():
                halos[cc].wait_recv()
        base = pl.multiple_of(c * cw, cw)
        for u in range(units):
            window = x_ref[u, pl.ds(base, cw + 2 * PAD), :]
            for j in range(TAPS):
                first = PAD + 2 * j - (TAPS - 1)
                at = (u // 2) * span + j * wide + (u % 2) * chans
                l_ref[:, at:at + chans] = window[first:first + cw, :]
        for p in range(pairs):
            d0, d1 = max(p - 1, 0), min(p + 1, pairs - 1)
            w0, w1 = d0 - p + 1, d1 - p + 2
            pre = jnp.dot(
                l_ref[:, d0 * span:(d1 + 1) * span],
                w_ref[w0:w1].reshape((w1 - w0) * span, wide),
                preferred_element_type=jnp.float32)
            hidden = jax.nn.gelu(pre, approximate=True).astype(jnp.bfloat16)
            for q in range(2):
                near = lax.dot_general(
                    head_t[...], hidden[:, q * chans:(q + 1) * chans],
                    (((1,), (1,)), ((), ())), preferred_element_type=jnp.float32)
                near = near.astype(jnp.bfloat16)
                for a in range(ANG):
                    ns_ref[c, a, 2 * p + q] = near[2 * a:2 * a + 2, :]

        def send(i, inner):
            near_copy(c, lax.rem(me + i, tiles)).start()
            return inner

        lax.fori_loop(1, tiles, send, 0)
        pltpu.make_async_copy(
            ns_ref.at[c, me // groups], nr_ref.at[c, me], near_own.at[c]).start()
        return carry

    lax.fori_loop(0, CHUNKS, conv_chunk, 0)

    for c in range(CHUNKS):
        pltpu.make_async_copy(
            ns_ref.at[c, me // groups], nr_ref.at[c, me], near_own.at[c]).wait()

        def arrive(i, carry):
            near_arrival(c, lax.rem(me + i, tiles)).wait_recv()
            return carry

        lax.fori_loop(1, tiles, arrive, 0)

        def place(t, carry):
            for i in range(BUNCH):
                for u in range(units):
                    at = i * units + u
                    pair = nr_ref[c, t * BUNCH + i, u].astype(jnp.float32)
                    ef_ref[0, t, at:at + 1, c * cw:(c + 1) * cw] = pair[0:1]
                    ef_ref[1, t, at:at + 1, c * cw:(c + 1) * cw] = pair[1:2]
            return carry

        lax.fori_loop(0, tiles // BUNCH, place, 0)
    rows = tiles * units
    real = ef_ref[0].reshape(rows, pixels).astype(jnp.bfloat16)
    imag = ef_ref[1].reshape(rows, pixels).astype(jnp.bfloat16)
    e_ref[0, 0:rows, :] = real
    e_ref[0, rows:, :] = imag
    e_ref[1, 0:rows, :] = -imag
    e_ref[1, rows:, :] = real

    weight = source_w[me // groups]
    for copy in g_copies:
        copy.wait()

    vw = 2 * chans

    def image(v, carry):
        at = pl.multiple_of(v * vw, vw)

        def one(k, inner):
            amp = jnp.dot(e_ref[0], g_ref[k, :, pl.ds(at, vw)], preferred_element_type=jnp.float32)
            amp += jnp.dot(e_ref[1], g_ref[k, :, pl.ds(pixels + at, vw)], preferred_element_type=jnp.float32)
            power = amp * amp
            s_ref[...] += power[0:rows] + power[rows:]
            return inner

        s_ref[...] = jnp.zeros_like(s_ref)
        lax.fori_loop(0, kers, one, 0)
        part = s_ref[...] * weight
        for t in range(tiles):
            for h in range(2):
                first = t * units + h * half
                r_ref[t, h, :, pl.ds(at, vw)] = part[first:first + half].astype(jnp.bfloat16)
        return carry

    lax.fori_loop(0, pixels // vw, image, 0)

    def ret_copy(h, peer):
        return pltpu.make_async_remote_copy(
            src_ref=r_ref.at[peer, h], dst_ref=rr_ref.at[sec, me],
            send_sem=ret_send.at[h, peer], recv_sem=ret_recv.at[sec, me],
            device_id=(h, peer), device_id_type=MESH)

    def ret_arrival(h, peer):
        return pltpu.make_async_remote_copy(
            src_ref=r_ref.at[peer, h], dst_ref=rr_ref.at[h, peer],
            send_sem=ret_send.at[h, peer], recv_sem=ret_recv.at[h, peer],
            device_id=(h, peer), device_id_type=MESH)

    def ret_go(i, carry):
        peer = lax.rem(me + i, tiles)
        ret_copy(sec, peer).start()
        ret_copy(1 - sec, peer).start()
        return carry

    ret_copy(1 - sec, me).start()
    lax.fori_loop(1, tiles, ret_go, 0)
    mine = pltpu.make_async_copy(r_ref.at[me, sec], rr_ref.at[sec, me], ret_own)
    mine.start()
    mine.wait()
    ret_arrival(1 - sec, me).wait()

    def ret_end(i, carry):
        peer = lax.rem(me + i, tiles)
        ret_arrival(sec, peer).wait()
        ret_arrival(1 - sec, peer).wait()
        return carry

    lax.fori_loop(1, tiles, ret_end, 0)

    for par in range(2):
        def gather(t, total):
            return total + rr_ref[par, t].astype(jnp.float32)

        total = lax.fori_loop(0, tiles, gather, jnp.zeros((half, pixels), jnp.float32))
        for j in range(half):
            out_ref[0, 2 * j + par:2 * j + par + 1, :] = total[j:j + 1]

    for copy in halos:
        copy.wait_send()
    for c in range(CHUNKS):
        def sent(i, carry):
            near_copy(c, lax.rem(me + i, tiles)).wait_send()
            return carry

        lax.fori_loop(1, tiles, sent, 0)


def on_device(features, conv_weight, head_weight, kernels, source_weights):
    tiles = lax.axis_size("tile")
    groups = tiles // ANG
    _, rows_dev, pixels, chans = features.shape
    half = rows_dev // 2
    units = 2 * half
    kers = kernels.shape[0]
    cw = pixels // CHUNKS
    bf16, f32 = jnp.bfloat16, jnp.float32
    feat = features.reshape(half, 2, pixels, chans)
    any_spec = pl.BlockSpec(memory_space=pl.ANY)
    return pl.pallas_call(
        functools.partial(kernel, tiles, groups),
        out_shape=jax.ShapeDtypeStruct((1, rows_dev, pixels), f32),
        in_specs=[
            any_spec,
            any_spec,
            pl.BlockSpec(memory_space=pltpu.VMEM),
            any_spec,
            pl.BlockSpec(memory_space=pltpu.SMEM),
        ],
        out_specs=pl.BlockSpec(memory_space=pltpu.VMEM),
        scratch_shapes=[
            pltpu.VMEM((units, pixels + 2 * PAD, chans), bf16),
            pltpu.VMEM((3, TAPS, 2 * chans, 2 * chans), bf16),
            pltpu.VMEM((cw, (units // 2) * TAPS * 2 * chans), bf16),
            pltpu.VMEM((CHUNKS, ANG, units, 2, cw), bf16),
            pltpu.VMEM((CHUNKS, tiles, units, 2, cw), bf16),
            pltpu.VMEM((2, tiles // BUNCH, BUNCH * units, pixels), f32),
            pltpu.VMEM((2, tiles * units * 2, pixels), bf16),
            pltpu.VMEM((kers, pixels, 2 * pixels), bf16),
            pltpu.VMEM((tiles * units, 2 * chans), f32),
            pltpu.VMEM((tiles, 2, half, pixels), bf16),
            pltpu.VMEM((2, tiles, half, pixels), bf16),
            pltpu.SemaphoreType.DMA,
            pltpu.SemaphoreType.DMA((10,)),
            pltpu.SemaphoreType.DMA((kers,)),
            pltpu.SemaphoreType.DMA((CHUNKS,)),
            pltpu.SemaphoreType.DMA((CHUNKS,)),
            pltpu.SemaphoreType.DMA((CHUNKS, tiles)),
            pltpu.SemaphoreType.DMA((CHUNKS, tiles)),
            pltpu.SemaphoreType.DMA((CHUNKS,)),
            pltpu.SemaphoreType.DMA((2, tiles)),
            pltpu.SemaphoreType.DMA((2, tiles)),
            pltpu.SemaphoreType.DMA,
        ],
        compiler_params=pltpu.CompilerParams(
            collective_id=0, has_side_effects=True, vmem_limit_bytes=66_000_000),
    )(feat, conv_weight, head_weight.T, kernels, source_weights)


def solution(mesh):
    in_specs = (P("tile", "section", None, None), P(), P(), P("tile", None, None), P())
    out_specs = P("tile", "section", None)
    return jax.shard_map(
        on_device, mesh=mesh, in_specs=in_specs, out_specs=out_specs, check_vma=False
    )
```

```python
import functools

import jax
import jax.numpy as jnp
from jax import lax
from jax.experimental import pallas as pl
from jax.experimental.pallas import tpu as pltpu
from jax.sharding import PartitionSpec as P

ANG = 8
TAPS = 5
CHUNKS = 4
PAD = 16
BUNCH = 4
SENDS = 2
MESH = pl.DeviceIdType.MESH


def kernel(tiles, groups, feat, conv_w, head_t, operators, source_w, out_ref,
           x_ref, w_ref, l_ref, ns_ref, nr_ref, ef_ref, e_ref, acc_ref, g_ref, s_ref, r_ref, rr_ref,
           own_sem, w_sem, g_sem, halo_send, halo_recv, near_send, near_recv, near_own,
           ret_send, ret_recv, ret_own):
    sec = lax.axis_index("section")
    me = lax.axis_index("tile")
    half, pixels, chans = feat.shape[0], feat.shape[2], feat.shape[3]
    units = 2 * half
    pairs = units // 2
    kers = operators.shape[0]
    cw = pixels // CHUNKS
    span = TAPS * 2 * chans
    wide = 2 * chans

    own = pltpu.make_async_copy(
        feat.at[:, sec], x_ref.at[pl.ds(sec * half, half), pl.ds(PAD, pixels), :], own_sem)
    own.start()
    w_copies = []
    for d in range(3):
        for si in range(2):
            for so in range(2):
                tap = 2 * d + si - so
                if 0 <= tap < TAPS:
                    copy = pltpu.make_async_copy(
                        conv_w.at[tap],
                        w_ref.at[d, :, pl.ds(si * chans, chans), pl.ds(so * chans, chans)],
                        w_sem.at[len(w_copies)])
                    copy.start()
                    w_copies.append(copy)
                else:
                    w_ref[d, :, si * chans:(si + 1) * chans, so * chans:(so + 1) * chans] = jnp.zeros(
                        (TAPS, chans, chans), w_ref.dtype)

    barrier = pltpu.get_barrier_semaphore()

    def greet(i, carry):
        peer = lax.rem(me + i, tiles)
        pl.semaphore_signal(barrier, inc=1, device_id=(sec, peer), device_id_type=MESH)
        pl.semaphore_signal(barrier, inc=1, device_id=(1 - sec, peer), device_id_type=MESH)
        return carry

    pl.semaphore_signal(barrier, inc=1, device_id=(1 - sec, me), device_id_type=MESH)
    lax.fori_loop(1, tiles, greet, 0)
    pl.semaphore_wait(barrier, 2 * tiles - 1)

    halos = []
    for c in range(CHUNKS):
        lo = 0 if c == 0 else c * cw + PAD
        hi = pixels if c == CHUNKS - 1 else (c + 1) * cw + PAD
        copy = pltpu.make_async_remote_copy(
            src_ref=feat.at[:, 1 - sec, pl.ds(lo, hi - lo), :],
            dst_ref=x_ref.at[pl.ds(sec * half, half), pl.ds(PAD + lo, hi - lo), :],
            send_sem=halo_send.at[c], recv_sem=halo_recv.at[c],
            device_id=(1 - sec, me), device_id_type=MESH)
        copy.start()
        halos.append(copy)

    g_copies = []
    for k in range(kers):
        copy = pltpu.make_async_copy(operators.at[k], g_ref.at[k], g_sem.at[k])
        copy.start()
        g_copies.append(copy)

    edge = jnp.zeros((units, PAD, chans), x_ref.dtype)
    x_ref[:, 0:PAD, :] = edge
    x_ref[:, PAD + pixels:, :] = edge
    own.wait()
    for copy in w_copies:
        copy.wait()

    def near_copy(c, peer):
        return pltpu.make_async_remote_copy(
            src_ref=ns_ref.at[c, peer // groups], dst_ref=nr_ref.at[c, me],
            send_sem=near_send.at[c, peer], recv_sem=near_recv.at[c, me],
            device_id=(sec, peer), device_id_type=MESH)

    def near_arrival(c, peer):
        return pltpu.make_async_remote_copy(
            src_ref=ns_ref.at[c, 0], dst_ref=nr_ref.at[c, peer],
            send_sem=near_send.at[c, peer], recv_sem=near_recv.at[c, peer],
            device_id=(sec, peer), device_id_type=MESH)

    def conv_chunk(c, carry):
        for cc in range(CHUNKS):
            @pl.when(c == cc)
            def _():
                halos[cc].wait_recv()
        base = pl.multiple_of(c * cw, cw)
        for u in range(units):
            window = x_ref[u, pl.ds(base, cw + 2 * PAD), :]
            for j in range(TAPS):
                first = PAD + 2 * j - (TAPS - 1)
                at = (u // 2) * span + j * wide + (u % 2) * chans
                l_ref[:, at:at + chans] = window[first:first + cw, :]
        for p in range(pairs):
            d0, d1 = max(p - 1, 0), min(p + 1, pairs - 1)
            w0, w1 = d0 - p + 1, d1 - p + 2
            pre = jnp.dot(
                l_ref[:, d0 * span:(d1 + 1) * span],
                w_ref[w0:w1].reshape((w1 - w0) * span, wide),
                preferred_element_type=jnp.float32)
            hidden = jax.nn.gelu(pre, approximate=True).astype(jnp.bfloat16)
            for q in range(2):
                near = lax.dot_general(
                    head_t[...], hidden[:, q * chans:(q + 1) * chans],
                    (((1,), (1,)), ((), ())), preferred_element_type=jnp.float32)
                near = near.astype(jnp.bfloat16)
                for a in range(ANG):
                    ns_ref[c, a, 2 * p + q] = near[2 * a:2 * a + 2, :]

        def send(i, inner):
            near_copy(c, lax.rem(me + i, tiles)).start()
            return inner

        lax.fori_loop(1, tiles, send, 0)
        pltpu.make_async_copy(
            ns_ref.at[c, me // groups], nr_ref.at[c, me], near_own.at[c]).start()
        return carry

    rows = tiles * units
    vw = 2 * chans
    part_v = pixels // vw
    per_send = part_v // SENDS
    weight = source_w[me // groups]

    def gather_chunk(c):
        pltpu.make_async_copy(
            ns_ref.at[c, me // groups], nr_ref.at[c, me], near_own.at[c]).wait()

        def arrive(i, inner):
            near_arrival(c, lax.rem(me + i, tiles)).wait_recv()
            return inner

        lax.fori_loop(1, tiles, arrive, 0)

        def place(t, inner):
            for i in range(BUNCH):
                for u in range(units):
                    at = i * units + u
                    pair = nr_ref[c, t * BUNCH + i, u].astype(jnp.float32)
                    ef_ref[0, t, at:at + 1, :] = pair[0:1]
                    ef_ref[1, t, at:at + 1, :] = pair[1:2]
            return inner

        lax.fori_loop(0, tiles // BUNCH, place, 0)
        real = ef_ref[0].reshape(rows, cw).astype(jnp.bfloat16)
        imag = ef_ref[1].reshape(rows, cw).astype(jnp.bfloat16)
        e_ref[0:rows, 0:cw] = real
        e_ref[rows:, 0:cw] = imag
        e_ref[0:rows, cw:] = -imag
        e_ref[rows:, cw:] = real

    def product(c, v, k):
        top = pl.multiple_of(c * cw, cw)
        at = pl.multiple_of(v * vw, vw)
        amp = jnp.dot(e_ref[:, 0:cw], g_ref[k, pl.ds(top, cw), pl.ds(at, vw)],
                      preferred_element_type=jnp.float32)
        return amp + jnp.dot(e_ref[:, cw:], g_ref[k, pl.ds(top, cw), pl.ds(pixels + at, vw)],
                             preferred_element_type=jnp.float32)

    def step(c, carry):
        @pl.when(c < CHUNKS)
        def _():
            conv_chunk(c, 0)

        @pl.when(c > 0)
        def _():
            gather_chunk(c - 1)

            def image(k, inner):
                @pl.when(c == 1)
                def _():
                    for kk in range(kers):
                        @pl.when(k == kk)
                        def _():
                            g_copies[kk].wait()

                for v in range(part_v):
                    acc_ref[k, v] += product(c - 1, v, k)
                return inner

            lax.fori_loop(0, kers, image, 0)
        return carry

    acc_ref[...] = jnp.zeros_like(acc_ref)
    lax.fori_loop(0, CHUNKS, step, 0)
    gather_chunk(CHUNKS - 1)

    def ret_copy(n, h, peer):
        return pltpu.make_async_remote_copy(
            src_ref=r_ref.at[n, peer, h], dst_ref=rr_ref.at[n, sec, me],
            send_sem=ret_send.at[n, h, peer], recv_sem=ret_recv.at[n, sec, me],
            device_id=(h, peer), device_id_type=MESH)

    def ret_arrival(n, h, peer):
        return pltpu.make_async_remote_copy(
            src_ref=r_ref.at[n, peer, h], dst_ref=rr_ref.at[n, h, peer],
            send_sem=ret_send.at[n, h, peer], recv_sem=ret_recv.at[n, h, peer],
            device_id=(h, peer), device_id_type=MESH)

    def ret_mine(n):
        return pltpu.make_async_copy(r_ref.at[n, me, sec], rr_ref.at[n, sec, me], ret_own.at[n])

    for n in range(SENDS):
        def last(k, inner):
            for m in range(per_send):
                v = n * per_send + m
                amp = acc_ref[k, v] + product(CHUNKS - 1, v, k)
                power = amp * amp
                s_ref[:, m * vw:(m + 1) * vw] += power[0:rows] + power[rows:]
            return inner

        s_ref[...] = jnp.zeros_like(s_ref)
        lax.fori_loop(0, kers, last, 0)
        part = s_ref[...] * weight
        for t in range(tiles):
            for h in range(2):
                first = t * units + h * half
                r_ref[n, t, h] = part[first:first + half].astype(jnp.bfloat16)

        def ret_go(i, carry):
            peer = lax.rem(me + i, tiles)
            ret_copy(n, sec, peer).start()
            ret_copy(n, 1 - sec, peer).start()
            return carry

        lax.fori_loop(1, tiles, ret_go, 0)
        ret_copy(n, 1 - sec, me).start()
        ret_mine(n).start()

    for n in range(SENDS):
        ret_mine(n).wait()
        ret_arrival(n, 1 - sec, me).wait()

        def ret_end(i, carry):
            peer = lax.rem(me + i, tiles)
            ret_arrival(n, sec, peer).wait()
            ret_arrival(n, 1 - sec, peer).wait()
            return carry

        lax.fori_loop(1, tiles, ret_end, 0)

        for par in range(2):
            def gather(t, total):
                return total + rr_ref[n, par, t].astype(jnp.float32)

            total = lax.fori_loop(0, tiles, gather, jnp.zeros((half, pixels // SENDS), jnp.float32))
            cols = slice(n * (pixels // SENDS), (n + 1) * (pixels // SENDS))
            for j in range(half):
                out_ref[0, 2 * j + par:2 * j + par + 1, cols] = total[j:j + 1]

    for copy in halos:
        copy.wait_send()
    for c in range(CHUNKS):
        def sent(i, carry):
            near_copy(c, lax.rem(me + i, tiles)).wait_send()
            return carry

        lax.fori_loop(1, tiles, sent, 0)


def on_device(features, conv_weight, head_weight, kernels, source_weights):
    tiles = lax.axis_size("tile")
    groups = tiles // ANG
    _, rows_dev, pixels, chans = features.shape
    half = rows_dev // 2
    units = 2 * half
    kers = kernels.shape[0]
    cw = pixels // CHUNKS
    bf16, f32 = jnp.bfloat16, jnp.float32
    feat = features.reshape(half, 2, pixels, chans)
    any_spec = pl.BlockSpec(memory_space=pl.ANY)
    return pl.pallas_call(
        functools.partial(kernel, tiles, groups),
        out_shape=jax.ShapeDtypeStruct((1, rows_dev, pixels), f32),
        in_specs=[
            any_spec,
            any_spec,
            pl.BlockSpec(memory_space=pltpu.VMEM),
            any_spec,
            pl.BlockSpec(memory_space=pltpu.SMEM),
        ],
        out_specs=pl.BlockSpec(memory_space=pltpu.VMEM),
        scratch_shapes=[
            pltpu.VMEM((units, pixels + 2 * PAD, chans), bf16),
            pltpu.VMEM((3, TAPS, 2 * chans, 2 * chans), bf16),
            pltpu.VMEM((cw, (units // 2) * TAPS * 2 * chans), bf16),
            pltpu.VMEM((CHUNKS, ANG, units, 2, cw), bf16),
            pltpu.VMEM((CHUNKS, tiles, units, 2, cw), bf16),
            pltpu.VMEM((2, tiles // BUNCH, BUNCH * units, cw), f32),
            pltpu.VMEM((tiles * units * 2, 2 * cw), bf16),
            pltpu.VMEM((kers, pixels // (2 * chans), tiles * units * 2, 2 * chans), f32),
            pltpu.VMEM((kers, pixels, 2 * pixels), bf16),
            pltpu.VMEM((tiles * units, pixels // SENDS), f32),
            pltpu.VMEM((SENDS, tiles, 2, half, pixels // SENDS), bf16),
            pltpu.VMEM((SENDS, 2, tiles, half, pixels // SENDS), bf16),
            pltpu.SemaphoreType.DMA,
            pltpu.SemaphoreType.DMA((10,)),
            pltpu.SemaphoreType.DMA((kers,)),
            pltpu.SemaphoreType.DMA((CHUNKS,)),
            pltpu.SemaphoreType.DMA((CHUNKS,)),
            pltpu.SemaphoreType.DMA((CHUNKS, tiles)),
            pltpu.SemaphoreType.DMA((CHUNKS, tiles)),
            pltpu.SemaphoreType.DMA((CHUNKS,)),
            pltpu.SemaphoreType.DMA((SENDS, 2, tiles)),
            pltpu.SemaphoreType.DMA((SENDS, 2, tiles)),
            pltpu.SemaphoreType.DMA((SENDS,)),
        ],
        compiler_params=pltpu.CompilerParams(
            collective_id=0, has_side_effects=True, vmem_limit_bytes=66_000_000),
    )(feat, conv_weight, head_weight.T, kernels, source_weights)


def solution(mesh):
    in_specs = (P("tile", "section", None, None), P(), P(), P("tile", None, None), P())
    out_specs = P("tile", "section", None)
    return jax.shard_map(
        on_device, mesh=mesh, in_specs=in_specs, out_specs=out_specs, check_vma=False
    )
```

```python
import functools

import jax
import jax.numpy as jnp
from jax import lax
from jax.experimental import pallas as pl
from jax.experimental.pallas import tpu as pltpu
from jax.sharding import PartitionSpec as P

ANG = 8
TAPS = 5
CHUNKS = 4
PAD = 16
BUNCH = 4
SENDS = 2
MESH = pl.DeviceIdType.MESH


def kernel(tiles, groups, feat, conv_w, head_t, operators, source_w, out_ref,
           x_ref, w_ref, l_ref, ns_ref, nr_ref, ef_ref, e_ref, acc_ref, g_ref, s_ref, r_ref, rr_ref,
           own_sem, w_sem, g_sem, halo_send, halo_recv, near_send, near_recv, near_own,
           ret_send, ret_recv, ret_own):
    sec = lax.axis_index("section")
    me = lax.axis_index("tile")
    half, pixels, chans = feat.shape[0], feat.shape[2], feat.shape[3]
    units = 2 * half
    pairs = units // 2
    kers = operators.shape[0]
    cw = pixels // CHUNKS
    span = TAPS * 2 * chans
    wide = 2 * chans

    own = pltpu.make_async_copy(
        feat.at[:, sec], x_ref.at[pl.ds(sec * half, half), pl.ds(PAD, pixels), :], own_sem)
    own.start()
    w_copies = []
    for d in range(3):
        for si in range(2):
            for so in range(2):
                tap = 2 * d + si - so
                if 0 <= tap < TAPS:
                    copy = pltpu.make_async_copy(
                        conv_w.at[tap],
                        w_ref.at[d, :, pl.ds(si * chans, chans), pl.ds(so * chans, chans)],
                        w_sem.at[len(w_copies)])
                    copy.start()
                    w_copies.append(copy)
                else:
                    w_ref[d, :, si * chans:(si + 1) * chans, so * chans:(so + 1) * chans] = jnp.zeros(
                        (TAPS, chans, chans), w_ref.dtype)

    barrier = pltpu.get_barrier_semaphore()

    def greet(i, carry):
        peer = lax.rem(me + i, tiles)
        pl.semaphore_signal(barrier, inc=1, device_id=(sec, peer), device_id_type=MESH)
        pl.semaphore_signal(barrier, inc=1, device_id=(1 - sec, peer), device_id_type=MESH)
        return carry

    pl.semaphore_signal(barrier, inc=1, device_id=(1 - sec, me), device_id_type=MESH)
    lax.fori_loop(1, tiles, greet, 0)
    pl.semaphore_wait(barrier, 2 * tiles - 1)

    halos = []
    for c in range(CHUNKS):
        lo = 0 if c == 0 else c * cw + PAD
        hi = pixels if c == CHUNKS - 1 else (c + 1) * cw + PAD
        copy = pltpu.make_async_remote_copy(
            src_ref=feat.at[:, 1 - sec, pl.ds(lo, hi - lo), :],
            dst_ref=x_ref.at[pl.ds(sec * half, half), pl.ds(PAD + lo, hi - lo), :],
            send_sem=halo_send.at[c], recv_sem=halo_recv.at[c],
            device_id=(1 - sec, me), device_id_type=MESH)
        copy.start()
        halos.append(copy)

    g_copies = []
    for k in range(kers):
        copy = pltpu.make_async_copy(operators.at[k], g_ref.at[k], g_sem.at[k])
        copy.start()
        g_copies.append(copy)

    edge = jnp.zeros((units, PAD, chans), x_ref.dtype)
    x_ref[:, 0:PAD, :] = edge
    x_ref[:, PAD + pixels:, :] = edge
    own.wait()
    for copy in w_copies:
        copy.wait()

    def near_copy(c, peer):
        return pltpu.make_async_remote_copy(
            src_ref=ns_ref.at[c, peer // groups], dst_ref=nr_ref.at[c, me],
            send_sem=near_send.at[c, peer], recv_sem=near_recv.at[c, me],
            device_id=(sec, peer), device_id_type=MESH)

    def near_arrival(c, peer):
        return pltpu.make_async_remote_copy(
            src_ref=ns_ref.at[c, 0], dst_ref=nr_ref.at[c, peer],
            send_sem=near_send.at[c, peer], recv_sem=near_recv.at[c, peer],
            device_id=(sec, peer), device_id_type=MESH)

    def conv_chunk(c, carry):
        for cc in range(CHUNKS):
            @pl.when(c == cc)
            def _():
                halos[cc].wait_recv()
        base = pl.multiple_of(c * cw, cw)
        def build(u):
            window = x_ref[u, pl.ds(base, cw + 2 * PAD), :]
            for j in range(TAPS):
                first = PAD + 2 * j - (TAPS - 1)
                at = (u // 2) * span + j * wide + (u % 2) * chans
                l_ref[:, at:at + chans] = window[first:first + cw, :]

        build(0)
        build(1)
        for p in range(pairs):
            if p + 1 < pairs:
                build(2 * p + 2)
                build(2 * p + 3)
            d0, d1 = max(p - 1, 0), min(p + 1, pairs - 1)
            w0, w1 = d0 - p + 1, d1 - p + 2
            pre = jnp.dot(
                l_ref[:, d0 * span:(d1 + 1) * span],
                w_ref[w0:w1].reshape((w1 - w0) * span, wide),
                preferred_element_type=jnp.float32)
            hidden = jax.nn.gelu(pre, approximate=True).astype(jnp.bfloat16)
            for q in range(2):
                near = lax.dot_general(
                    head_t[...], hidden[:, q * chans:(q + 1) * chans],
                    (((1,), (1,)), ((), ())), preferred_element_type=jnp.float32)
                near = near.astype(jnp.bfloat16)
                for a in range(ANG):
                    ns_ref[c, a, 2 * p + q] = near[2 * a:2 * a + 2, :]

        def send(i, inner):
            near_copy(c, lax.rem(me + i, tiles)).start()
            return inner

        lax.fori_loop(1, tiles, send, 0)
        pltpu.make_async_copy(
            ns_ref.at[c, me // groups], nr_ref.at[c, me], near_own.at[c]).start()
        return carry

    rows = tiles * units
    vw = 2 * chans
    part_v = pixels // vw
    per_send = part_v // SENDS
    unroll = 4 if kers % 4 == 0 else 1
    weight = source_w[me // groups]

    def gather_chunk(c):
        pltpu.make_async_copy(
            ns_ref.at[c, me // groups], nr_ref.at[c, me], near_own.at[c]).wait()

        def arrive(i, inner):
            near_arrival(c, lax.rem(me + i, tiles)).wait_recv()
            return inner

        lax.fori_loop(1, tiles, arrive, 0)

        def place(t, inner):
            for i in range(BUNCH):
                for u in range(units):
                    at = i * units + u
                    pair = nr_ref[c, t * BUNCH + i, u].astype(jnp.float32)
                    ef_ref[0, t, at:at + 1, :] = pair[0:1]
                    ef_ref[1, t, at:at + 1, :] = pair[1:2]
            return inner

        lax.fori_loop(0, tiles // BUNCH, place, 0)
        real = ef_ref[0].reshape(rows, cw).astype(jnp.bfloat16)
        imag = ef_ref[1].reshape(rows, cw).astype(jnp.bfloat16)
        e_ref[0:rows, 0:cw] = real
        e_ref[rows:, 0:cw] = imag
        e_ref[0:rows, cw:] = -imag
        e_ref[rows:, cw:] = real

    def product(c, v, k):
        top = pl.multiple_of(c * cw, cw)
        at = pl.multiple_of(v * vw, vw)
        amp = jnp.dot(e_ref[:, 0:cw], g_ref[k, pl.ds(top, cw), pl.ds(at, vw)],
                      preferred_element_type=jnp.float32)
        return amp + jnp.dot(e_ref[:, cw:], g_ref[k, pl.ds(top, cw), pl.ds(pixels + at, vw)],
                             preferred_element_type=jnp.float32)

    def step(c, carry):
        @pl.when(c < CHUNKS)
        def _():
            conv_chunk(c, 0)

        @pl.when(c > 0)
        def _():
            gather_chunk(c - 1)

            @pl.when(c == 1)
            def _():
                for copy in g_copies:
                    copy.wait()

            def image(kb, inner):
                for i in range(unroll):
                    for v in range(part_v):
                        acc_ref[kb * unroll + i, v] += product(c - 1, v, kb * unroll + i)
                return inner

            lax.fori_loop(0, kers // unroll, image, 0)
        return carry

    acc_ref[...] = jnp.zeros_like(acc_ref)
    lax.fori_loop(0, CHUNKS, step, 0)
    gather_chunk(CHUNKS - 1)

    def ret_copy(n, h, peer):
        return pltpu.make_async_remote_copy(
            src_ref=r_ref.at[n, peer, h], dst_ref=rr_ref.at[n, sec, me],
            send_sem=ret_send.at[n, h, peer], recv_sem=ret_recv.at[n, sec, me],
            device_id=(h, peer), device_id_type=MESH)

    def ret_arrival(n, h, peer):
        return pltpu.make_async_remote_copy(
            src_ref=r_ref.at[n, peer, h], dst_ref=rr_ref.at[n, h, peer],
            send_sem=ret_send.at[n, h, peer], recv_sem=ret_recv.at[n, h, peer],
            device_id=(h, peer), device_id_type=MESH)

    def ret_mine(n):
        return pltpu.make_async_copy(r_ref.at[n, me, sec], rr_ref.at[n, sec, me], ret_own.at[n])

    for n in range(SENDS):
        def last(kb, inner):
            for i in range(unroll):
                k = kb * unroll + i
                for m in range(per_send):
                    v = n * per_send + m
                    amp = acc_ref[k, v] + product(CHUNKS - 1, v, k)
                    power = amp * amp
                    s_ref[:, m * vw:(m + 1) * vw] += power[0:rows] + power[rows:]
            return inner

        s_ref[...] = jnp.zeros_like(s_ref)
        lax.fori_loop(0, kers // unroll, last, 0)
        part = s_ref[...] * weight
        for t in range(tiles):
            for h in range(2):
                first = t * units + h * half
                r_ref[n, t, h] = part[first:first + half].astype(jnp.bfloat16)

        def ret_go(i, carry):
            peer = lax.rem(me + i, tiles)
            ret_copy(n, sec, peer).start()
            ret_copy(n, 1 - sec, peer).start()
            return carry

        lax.fori_loop(1, tiles, ret_go, 0)
        ret_copy(n, 1 - sec, me).start()
        ret_mine(n).start()

    for n in range(SENDS):
        ret_mine(n).wait()
        ret_arrival(n, 1 - sec, me).wait()

        def ret_end(i, carry):
            peer = lax.rem(me + i, tiles)
            ret_arrival(n, sec, peer).wait()
            ret_arrival(n, 1 - sec, peer).wait()
            return carry

        lax.fori_loop(1, tiles, ret_end, 0)

        for par in range(2):
            def gather(t, total):
                return total + rr_ref[n, par, t].astype(jnp.float32)

            total = lax.fori_loop(0, tiles, gather, jnp.zeros((half, pixels // SENDS), jnp.float32))
            cols = slice(n * (pixels // SENDS), (n + 1) * (pixels // SENDS))
            for j in range(half):
                out_ref[0, 2 * j + par:2 * j + par + 1, cols] = total[j:j + 1]

    for copy in halos:
        copy.wait_send()
    for c in range(CHUNKS):
        def sent(i, carry):
            near_copy(c, lax.rem(me + i, tiles)).wait_send()
            return carry

        lax.fori_loop(1, tiles, sent, 0)


def on_device(features, conv_weight, head_weight, kernels, source_weights):
    tiles = lax.axis_size("tile")
    groups = tiles // ANG
    _, rows_dev, pixels, chans = features.shape
    half = rows_dev // 2
    units = 2 * half
    kers = kernels.shape[0]
    cw = pixels // CHUNKS
    bf16, f32 = jnp.bfloat16, jnp.float32
    feat = features.reshape(half, 2, pixels, chans)
    any_spec = pl.BlockSpec(memory_space=pl.ANY)
    return pl.pallas_call(
        functools.partial(kernel, tiles, groups),
        out_shape=jax.ShapeDtypeStruct((1, rows_dev, pixels), f32),
        in_specs=[
            any_spec,
            any_spec,
            pl.BlockSpec(memory_space=pltpu.VMEM),
            any_spec,
            pl.BlockSpec(memory_space=pltpu.SMEM),
        ],
        out_specs=pl.BlockSpec(memory_space=pltpu.VMEM),
        scratch_shapes=[
            pltpu.VMEM((units, pixels + 2 * PAD, chans), bf16),
            pltpu.VMEM((3, TAPS, 2 * chans, 2 * chans), bf16),
            pltpu.VMEM((cw, (units // 2) * TAPS * 2 * chans), bf16),
            pltpu.VMEM((CHUNKS, ANG, units, 2, cw), bf16),
            pltpu.VMEM((CHUNKS, tiles, units, 2, cw), bf16),
            pltpu.VMEM((2, tiles // BUNCH, BUNCH * units, cw), f32),
            pltpu.VMEM((tiles * units * 2, 2 * cw), bf16),
            pltpu.VMEM((kers, pixels // (2 * chans), tiles * units * 2, 2 * chans), f32),
            pltpu.VMEM((kers, pixels, 2 * pixels), bf16),
            pltpu.VMEM((tiles * units, pixels // SENDS), f32),
            pltpu.VMEM((SENDS, tiles, 2, half, pixels // SENDS), bf16),
            pltpu.VMEM((SENDS, 2, tiles, half, pixels // SENDS), bf16),
            pltpu.SemaphoreType.DMA,
            pltpu.SemaphoreType.DMA((10,)),
            pltpu.SemaphoreType.DMA((kers,)),
            pltpu.SemaphoreType.DMA((CHUNKS,)),
            pltpu.SemaphoreType.DMA((CHUNKS,)),
            pltpu.SemaphoreType.DMA((CHUNKS, tiles)),
            pltpu.SemaphoreType.DMA((CHUNKS, tiles)),
            pltpu.SemaphoreType.DMA((CHUNKS,)),
            pltpu.SemaphoreType.DMA((SENDS, 2, tiles)),
            pltpu.SemaphoreType.DMA((SENDS, 2, tiles)),
            pltpu.SemaphoreType.DMA((SENDS,)),
        ],
        compiler_params=pltpu.CompilerParams(
            collective_id=0, has_side_effects=True, vmem_limit_bytes=66_000_000),
    )(feat, conv_weight, head_weight.T, kernels, source_weights)


def solution(mesh):
    in_specs = (P("tile", "section", None, None), P(), P(), P("tile", None, None), P())
    out_specs = P("tile", "section", None)
    return jax.shard_map(
        on_device, mesh=mesh, in_specs=in_specs, out_specs=out_specs, check_vma=False
    )
```
